32 devices in a mesh: img: 16 (over z, y, x), blk: 2 (over core).
Axes of the slice: x: 2, y: 2, z: 4, core: 2. Of those that a mesh axis runs over, the one named last changes fastest.
Arguments:
- descriptors: bfloat16 [64, 128, 256], P(('img', 'blk')), may hold values from -8 to 8
- covisible: int32 [64, 6], P(('img', 'blk')), may hold values from 0 to 63, as said below
- tile_counts: int32 [64], P(('img', 'blk')), may hold values from 1 to 6, as said below
- keypoints: int32 [64], replicated, may hold values from 32 to 128, as said below
- query_weight: bfloat16 [256, 256], replicated, may hold values from -0.375 to 0.375
- key_weight: bfloat16 [256, 256], replicated, may hold values from -0.375 to 0.375
- value_weight: bfloat16 [256, 256], replicated, may hold values from -0.375 to 0.375
- merge_weight: bfloat16 [512, 512], replicated, may hold values from -0.25 to 0.25
- output_weight: bfloat16 [512, 256], replicated, may hold values from -0.25 to 0.25
- dustbin: float32 [1], replicated, may hold values from 0.5 to 2
Outputs:
- plan: float32 [64, 6, 128, 128], P(('img', 'blk'))
- row_bin: float32 [64, 128], P(('img', 'blk'))
- col_bin: float32 [64, 128], P(('img', 'blk'))
The draws below stay inside these ranges and needn't reach their ends.
Inputs may be any that keep to these rules, and one draw needn't show every extreme that they name: `covisible`: the 6 entries of a block's row name different blocks, never the block itself, all within its own image group of 4 consecutive blocks or the groups just before and after it. `tile_counts`: some block uses all 6 of its listed blocks. The valid keypoints of a block are its first ones; some block is full.
All inputs are finite; a program needn't handle non-finite values.
Results may differ from the reference program's by a relative error of at most 0.0032.
Values may be sent and summed in bfloat16 or wider, within the bound.
A program may use at most 64 MiB of HBM per device.

```python
import math
import jax
import jax.numpy as jnp
from jax import lax

D = 256
HEADS = 4
BLOCK = 128
TILES = 6
ITERS = 3
GROUP = 4
NB = 64


def draw_descriptors(key, part):
    drawn_key = jax.random.fold_in(key, 101)
    return jnp.clip(jax.random.normal(drawn_key, (NB, BLOCK, D), jnp.float32), -8.0, 8.0).astype(jnp.bfloat16)


def draw_covisible(key, part):
    rows = jnp.arange(NB, dtype=jnp.int32)
    groups = rows // GROUP
    slots = jnp.arange(3 * GROUP, dtype=jnp.int32)
    candidate = (groups[:, None] - 1) * GROUP + slots[None, :]
    usable = (candidate >= 0) & (candidate < NB) & (candidate != rows[:, None])
    ranks = jax.vmap(lambda sub: jax.random.permutation(sub, 3 * GROUP))(jax.random.split(jax.random.fold_in(key, 201), NB))
    ranking = ranks.astype(jnp.int32) + jnp.where(usable, 0, 3 * GROUP)
    order = jnp.argsort(ranking, axis=1, stable=True)[:, :TILES]
    return jnp.take_along_axis(candidate, order, axis=1).astype(jnp.int32)


def draw_tile_counts(key, part):
    rows = jnp.arange(NB, dtype=jnp.int32)
    drawn = jax.random.randint(jax.random.fold_in(key, 301), (NB,), 1, TILES + 1)
    return jnp.where(rows % 5 == 0, TILES, drawn).astype(jnp.int32)


def draw_keypoints(key, part):
    rows = jnp.arange(NB, dtype=jnp.int32)
    drawn = jax.random.randint(jax.random.fold_in(key, 401), (NB,), BLOCK // 4, BLOCK + 1)
    return jnp.where(rows % 3 == 0, BLOCK, drawn).astype(jnp.int32)


def normal_values(rng, extent, spread, limit, held_as=jnp.bfloat16):
    return jnp.clip(spread * jax.random.normal(rng, extent, jnp.float32), -limit, limit).astype(held_as)


def setup_inputs(seed: int = 0) -> dict:
    splits = jax.random.split(jax.random.key(seed), 11)
    return {
        "descriptors": draw_descriptors(jax.random.fold_in(splits[10], 71), 0),
        "covisible": draw_covisible(jax.random.fold_in(splits[10], 71), 0),
        "tile_counts": draw_tile_counts(jax.random.fold_in(splits[10], 71), 0),
        "keypoints": draw_keypoints(jax.random.fold_in(splits[10], 71), 0),
        "query_weight": normal_values(splits[4], (D, D), D ** -0.5, 0.375),
        "key_weight": normal_values(splits[5], (D, D), D ** -0.5, 0.375),
        "value_weight": normal_values(splits[6], (D, D), D ** -0.5, 0.375),
        "merge_weight": normal_values(splits[7], (2 * D, 2 * D), (2 * D) ** -0.5, 0.25),
        "output_weight": normal_values(splits[8], (2 * D, D), (2 * D) ** -0.5, 0.25),
        "dustbin": jnp.clip(jax.random.uniform(splits[9], (1,), jnp.float32, 0.5, 2.0), 0.5, 2.0),
    }


def project_rows(values, weight):
    flat = jnp.dot(values.reshape(-1, values.shape[-1]), weight, preferred_element_type=jnp.float32)
    return flat.reshape(values.shape[:-1] + (weight.shape[1],)).astype(jnp.bfloat16)

def reference(descriptors, covisible, tile_counts, keypoints, query_weight, key_weight, value_weight, merge_weight, output_weight, dustbin):
    block_count, block_len, feature_dim = descriptors.shape
    head_dim = feature_dim // HEADS
    tile_count = covisible.shape[1]
    query = project_rows(descriptors, query_weight)
    keys_all = project_rows(descriptors, key_weight)
    values_all = project_rows(descriptors, value_weight)
    tile_slots = jnp.arange(tile_count, dtype=jnp.int32)
    positions = jnp.arange(block_len, dtype=jnp.int32)

    def attend(pieces):
        query_block, own_block, row_cols, count = pieces
        key_tiles = keys_all[row_cols].reshape(tile_count * block_len, HEADS, head_dim).astype(jnp.float32)
        value_tiles = values_all[row_cols].reshape(tile_count * block_len, HEADS, head_dim).astype(jnp.float32)
        key_live = (tile_slots[:, None] < count) & (positions[None, :] < keypoints[row_cols][:, None])
        logits = jnp.einsum('qhd,khd->hqk', query_block.reshape(block_len, HEADS, head_dim).astype(jnp.float32), key_tiles) / math.sqrt(head_dim)
        logits = jnp.where(key_live.reshape(1, 1, -1), logits, -1e+30)
        highest = lax.optimization_barrier(jnp.max(logits, axis=2, keepdims=True))
        weights = jnp.exp(logits - highest)
        weights = (weights / lax.optimization_barrier(jnp.sum(weights, axis=2, keepdims=True))).astype(jnp.bfloat16)
        message = jnp.einsum('hqk,khd->qhd', weights.astype(jnp.float32), value_tiles).reshape(block_len, feature_dim).astype(jnp.bfloat16)
        joined = jnp.concatenate([own_block, message], axis=1)
        hidden = jnp.maximum(jnp.dot(joined, merge_weight, preferred_element_type=jnp.float32), 0.0).astype(jnp.bfloat16)
        return (own_block.astype(jnp.float32) + jnp.dot(hidden, output_weight, preferred_element_type=jnp.float32)).astype(jnp.bfloat16)
    refined = lax.map(attend, (query, descriptors, covisible, tile_counts))

    def score_tiles(pieces):
        own_block, row_cols = pieces
        other = refined[row_cols].astype(jnp.float32)
        return jnp.einsum('id,kjd->kij', own_block.astype(jnp.float32), other) / math.sqrt(feature_dim)
    scores = lax.map(score_tiles, (refined, covisible))
    row_live = positions[None, :] < keypoints[:, None]
    tile_live = tile_slots[None, :] < tile_counts[:, None]
    col_live = row_live[covisible]
    valid = tile_live[:, :, None, None] & row_live[:, None, :, None] & col_live[:, :, None, :]
    dust = dustbin[0]
    col_pot = jnp.zeros((block_count, block_len), jnp.float32)
    row_pot = jnp.zeros((block_count, block_len), jnp.float32)
    for sweep in range(ITERS):
        tile_pot = col_pot[covisible]
        shifted = jnp.where(valid, scores + tile_pot[:, :, None, :], -1e+30)
        highest = jnp.maximum(lax.optimization_barrier(jnp.max(shifted, axis=(1, 3))), dust)
        total = lax.optimization_barrier(jnp.sum(jnp.exp(shifted - highest[:, None, :, None]), axis=(1, 3))) + jnp.exp(dust - highest)
        row_pot = -(highest + jnp.log(total))
        mass = lax.optimization_barrier(jnp.sum(jnp.where(valid, jnp.exp(scores + row_pot[:, None, :, None] + tile_pot[:, :, None, :]), 0.0), axis=2))
        col_sum = jax.ops.segment_sum(mass.reshape(block_count * tile_count, block_len), covisible.reshape(-1), num_segments=block_count)
        col_pot = col_pot - jnp.log(col_sum + jnp.exp(dust + col_pot))
    tile_pot = col_pot[covisible]
    plan = jnp.where(valid, scores + row_pot[:, None, :, None] + tile_pot[:, :, None, :], 0.0)
    row_bin = jnp.where(row_live, dust + row_pot, 0.0)
    col_bin = jnp.where(row_live, dust + col_pot, 0.0)
    return (plan, row_bin, col_bin)
```

```python
import functools
import math

import jax
import jax.numpy as jnp
from jax import lax
from jax.experimental import pallas as pl
from jax.experimental.pallas import tpu as pltpu
from jax.sharding import PartitionSpec as P

HEADS = 4
ITERS = 3
DEAD = -1e30
MESH = pl.DeviceIdType.MESH


def kernel(
    img_count,
    blk_count,
    desc_ref,
    cov_ref,
    count_ref,
    kpt_ref,
    wq_ref,
    wk_ref,
    wv_ref,
    wm_ref,
    wo_ref,
    dust_ref,
    plan_ref,
    row_ref,
    col_ref,
    near_desc,
    near_ref,
    near_k,
    near_v,
    query,
    merged,
    scores,
    acc,
    mass_in,
    pot,
    desc_ssem,
    desc_rsem,
    ref_ssem,
    ref_rsem,
    mass_ssem,
    mass_rsem,
):
    local, block, width = desc_ref.shape
    tiles = cov_ref.shape[1]
    group = local * blk_count
    head_dim = width // HEADS
    img = lax.axis_index("img")
    blk = lax.axis_index("blk")
    others = [lax.rem(blk + step, blk_count) for step in range(1, blk_count)]
    first_block = (img - 1) * group

    def exists(shift):
        if shift == 0:
            return True
        return img + shift < img_count if shift > 0 else img + shift >= 0

    def guarded(shift, body):
        if shift == 0:
            body()
        else:
            pl.when(exists(shift))(body)

    barrier = pltpu.get_barrier_semaphore()
    for shift in range(-2, 3):
        def greet(shift=shift):
            for member in others if shift == 0 else range(blk_count):
                pl.semaphore_signal(
                    barrier, inc=1, device_id=(img + shift, member), device_id_type=MESH
                )
        guarded(shift, greet)

    def slot(near, section, member):
        return near.at[pl.ds((section * blk_count + member) * local, local)]

    def sender(source, near, ssem, rsem, section, shift, member):
        return pltpu.make_async_remote_copy(
            src_ref=source,
            dst_ref=slot(near, section, blk),
            send_sem=ssem.at[section, member],
            recv_sem=rsem.at[section, blk],
            device_id=(img + shift, member),
            device_id_type=MESH,
        )

    def arrival(near, ssem, rsem, section, member):
        here = slot(near, section, member)
        return pltpu.make_async_remote_copy(
            src_ref=here,
            dst_ref=here,
            send_sem=ssem.at[section, member],
            recv_sem=rsem.at[section, member],
            device_id=(img, others[0]),
            device_id_type=MESH,
        )

    def send_own(source, near, ssem, rsem):
        for shift in (1, -1):
            guarded(
                shift,
                lambda shift=shift: sender(
                    source, near, ssem, rsem, 1 - shift, shift, blk
                ).start(),
            )
        for member in others:
            sender(source, near, ssem, rsem, 1, 0, member).start()

    def relay(near, ssem, rsem, section):
        def body():
            arrival(near, ssem, rsem, section, blk).wait_recv()
            for member in others:
                sender(slot(near, section, blk), near, ssem, rsem, section, 0, member).start()
        guarded(section - 1, body)

    def wait_relayed(near, ssem, rsem, section, after=None):
        def body():
            for member in others:
                arrival(near, ssem, rsem, section, member).wait_recv()
                if after is not None:
                    after(section, member)
        guarded(section - 1, body)

    def drain(source, near, ssem, rsem):
        for shift in (1, -1):
            guarded(
                shift,
                lambda shift=shift: sender(
                    source, near, ssem, rsem, 1 - shift, shift, blk
                ).wait_send(),
            )
        for section in range(3):
            def body(section=section):
                for member in others:
                    sender(source, near, ssem, rsem, section, 0, member).wait_send()
            guarded(section - 1, body)

    def project(rows, section, member):
        where_to = pl.ds((section * blk_count + member) * local, local)
        for weight, target in ((wk_ref, near_k), (wv_ref, near_v)):
            out = jnp.dot(rows, weight[...], preferred_element_type=jnp.float32)
            target[where_to] = out.astype(jnp.bfloat16).reshape(local, block, width)

    def project_near(section, member):
        rows = near_desc[pl.ds((section * blk_count + member) * local, local)]
        project(rows.reshape(local * block, width), section, member)

    for source in range(-2, 3):
        if source != 0:
            @pl.when(jnp.logical_not(exists(source)))
            def _(source=source):
                for sweep in range(ITERS):
                    mass_in[sweep, source + 2] = jnp.zeros(mass_in.shape[2:], jnp.float32)

    own = desc_ref[...].reshape(local * block, width)
    low = jnp.maximum(img - 2, 0)
    high = jnp.minimum(img + 2, img_count - 1)
    pl.semaphore_wait(barrier, (high - low + 1) * blk_count - 1)
    send_own(desc_ref, near_desc, desc_ssem, desc_rsem)

    scaled = jnp.dot(own, wq_ref[...], preferred_element_type=jnp.float32) * (
        1.0 / math.sqrt(head_dim)
    )
    query[...] = scaled.astype(jnp.bfloat16).reshape(local, block, width)
    project(own, 1, blk)
    merged[...] = jnp.dot(
        own, wm_ref[pl.ds(0, width), :], preferred_element_type=jnp.float32
    ).reshape(merged.shape)
    wait_relayed(near_desc, desc_ssem, desc_rsem, 1, project_near)
    for section in (0, 2):
        relay(near_desc, desc_ssem, desc_rsem, section)
    for section in (0, 2):
        guarded(section - 1, lambda section=section: project_near(section, blk))
    for section in (0, 2):
        wait_relayed(near_desc, desc_ssem, desc_rsem, section, project_near)

    lanes = lax.broadcasted_iota(jnp.int32, (1, block), 1)
    rows_at = lax.broadcasted_iota(jnp.int32, (block, 1), 0)
    head_of = lax.broadcasted_iota(jnp.int32, (1, width), 1) // head_dim
    heads = [head_of == head for head in range(HEADS)]
    own_kpt = [kpt_ref[(img * blk_count + blk) * local + r] for r in range(local)]
    near_ids = [
        [jnp.clip(cov_ref[r, t] - first_block, 0, 3 * group - 1) for t in range(tiles)]
        for r in range(local)
    ]
    limits = [
        [
            jnp.where(t < count_ref[r], kpt_ref[jnp.clip(cov_ref[r, t], 0, kpt_ref.shape[0] - 1)], 0)
            for t in range(tiles)
        ]
        for r in range(local)
    ]
    biases = [
        [jnp.where(lanes < limits[r][t], 0.0, DEAD) for t in range(tiles)] for r in range(local)
    ]

    for r in range(local):
        keys = jnp.concatenate([near_k[near_ids[r][t]] for t in range(tiles)], axis=0)
        values = jnp.concatenate([near_v[near_ids[r][t]] for t in range(tiles)], axis=0)
        q = query[r]
        bias = jnp.concatenate(biases[r], axis=1)
        message = jnp.zeros((block, width), jnp.float32)
        for head in range(HEADS):
            logits = lax.dot_general(
                jnp.where(heads[head], q, jnp.zeros_like(q)),
                keys,
                (((1,), (1,)), ((), ())),
                preferred_element_type=jnp.float32,
            ) + bias
            weights = jnp.exp(logits - jnp.max(logits, axis=1, keepdims=True))
            weights = weights * (1.0 / jnp.sum(weights, axis=1, keepdims=True))
            out = jnp.dot(
                weights.astype(jnp.bfloat16), values, preferred_element_type=jnp.float32
            )
            message = jnp.where(heads[head], out, message)
        hidden = jnp.maximum(
            merged[r]
            + jnp.dot(
                message.astype(jnp.bfloat16),
                wm_ref[pl.ds(width, width), :],
                preferred_element_type=jnp.float32,
            ),
            0.0,
        ).astype(jnp.bfloat16)
        refined = desc_ref[r].astype(jnp.float32) + jnp.dot(
            hidden, wo_ref[...], preferred_element_type=jnp.float32
        )
        near_ref[group + blk * local + r] = refined.astype(jnp.bfloat16)

    own_slot = slot(near_ref, 1, blk)
    send_own(own_slot, near_ref, ref_ssem, ref_rsem)
    drain(desc_ref, near_desc, desc_ssem, desc_rsem)
    for section in (0, 2):
        relay(near_ref, ref_ssem, ref_rsem, section)
    for section in (1, 0, 2):
        wait_relayed(near_ref, ref_ssem, ref_rsem, section)

    dust = dust_ref[0]
    row_live = [rows_at < own_kpt[r] for r in range(local)]
    for r in range(local):
        mine = near_ref[group + blk * local + r] * jnp.asarray(
            1.0 / math.sqrt(width), jnp.bfloat16
        )
        row_bias = jnp.where(row_live[r], 0.0, DEAD)
        for t in range(tiles):
            out = lax.dot_general(
                mine,
                near_ref[near_ids[r][t]],
                (((1,), (1,)), ((), ())),
                preferred_element_type=jnp.float32,
            )
            scores[r, t] = out + (row_bias + biases[r][t])

    slots = lax.broadcasted_iota(jnp.int32, (group, 1), 0)
    pots = [jnp.zeros((group, block), jnp.float32)] * 3

    def mass_copy(sweep, shift, member):
        first, count = max(0, shift), 3 - abs(shift)
        return pltpu.make_async_remote_copy(
            src_ref=acc.at[sweep, pl.ds(first, count)],
            dst_ref=mass_in.at[sweep, 2 - shift, blk, pl.ds(first, count)],
            send_sem=mass_ssem.at[sweep, shift + 2, member],
            recv_sem=mass_rsem.at[sweep, 2 - shift, blk],
            device_id=(img + shift, member),
            device_id_type=MESH,
        )

    def mass_arrival(sweep, source, member):
        first, count = max(0, -source), 3 - abs(source)
        here = mass_in.at[sweep, source + 2, member, pl.ds(first, count)]
        return pltpu.make_async_remote_copy(
            src_ref=here,
            dst_ref=here,
            send_sem=mass_ssem.at[sweep, source + 2, member],
            recv_sem=mass_rsem.at[sweep, source + 2, member],
            device_id=(img, others[0]),
            device_id_type=MESH,
        )

    def each_partner(body):
        for shift in (-1, 1, -2, 2, 0):
            def run(shift=shift):
                for member in others if shift == 0 else range(blk_count):
                    body(shift, member)
            guarded(shift, run)

    row_pots = [None] * local
    for sweep in range(ITERS):
        spread = [jnp.zeros((group, block), jnp.float32)] * 3
        for r in range(local):
            def shifted(t):
                if sweep == 0:
                    return scores[r, t]
                return scores[r, t] + pot[pl.ds(near_ids[r][t], 1), :]
            top = shifted(0)
            for t in range(1, tiles):
                top = jnp.maximum(top, shifted(t))
            top = jnp.maximum(jnp.max(top, axis=1, keepdims=True), dust)
            terms = [jnp.exp(shifted(t) - top) for t in range(tiles)]
            total = functools.reduce(jnp.add, terms)
            total = jnp.sum(total, axis=1, keepdims=True) + jnp.exp(dust - top)
            row_pots[r] = -(top + jnp.log(total))
            inverse = 1.0 / total
            for t in range(tiles):
                mass = jnp.sum(terms[t] * inverse, axis=0, keepdims=True)
                for section in range(3):
                    hit = slots == near_ids[r][t] - section * group
                    spread[section] = spread[section] + jnp.where(hit, mass, 0.0)
        for section in range(3):
            acc[sweep, section] = spread[section]
        each_partner(lambda shift, member: mass_copy(sweep, shift, member).start())
        if sweep == 0:
            drain(own_slot, near_ref, ref_ssem, ref_rsem)
        if sweep == ITERS - 1:
            for r in range(local):
                row = jnp.broadcast_to(row_pots[r], (block, block))
                row = jnp.sum(jnp.where(rows_at == lanes, row, 0.0), axis=0, keepdims=True)
                row_ref[pl.ds(r, 1), :] = jnp.where(lanes < own_kpt[r], dust + row, 0.0)
                for t in range(tiles):
                    scores[r, t] = scores[r, t] + row_pots[r]
        sums = list(spread)
        each_partner(lambda source, member: mass_arrival(sweep, source, member).wait_recv())
        for source in range(-2, 3):
            for member in others if source == 0 else range(blk_count):
                for section in range(3):
                    if 0 <= section - source <= 2:
                        sums[section] = sums[section] + mass_in[
                            sweep, source + 2, member, section - source
                        ]
        for section in range(3):
            pots[section] = pots[section] - jnp.log(
                sums[section] + jnp.exp(dust + pots[section])
            )
            pot[pl.ds(section * group, group), :] = pots[section]

    for r in range(local):
        for t in range(tiles):
            out = scores[r, t] + pot[pl.ds(near_ids[r][t], 1), :]
            valid = jnp.where(row_live[r], lanes, block) < limits[r][t]
            plan_ref[r, t] = jnp.where(valid, out, 0.0)
        mine = pot[pl.ds(group + blk * local + r, 1), :]
        col_ref[pl.ds(r, 1), :] = jnp.where(lanes < own_kpt[r], dust + mine, 0.0)
    for sweep in range(ITERS):
        each_partner(lambda shift, member: mass_copy(sweep, shift, member).wait_send())


def on_device(
    img_count,
    blk_count,
    descriptors,
    covisible,
    tile_counts,
    keypoints,
    query_weight,
    key_weight,
    value_weight,
    merge_weight,
    output_weight,
    dustbin,
):
    local, block, width = descriptors.shape
    tiles = covisible.shape[1]
    group = local * blk_count
    near = 3 * group
    vmem = pl.BlockSpec(memory_space=pltpu.VMEM)
    smem = pl.BlockSpec(memory_space=pltpu.SMEM)
    dma = pltpu.SemaphoreType.DMA
    half = jnp.bfloat16
    full = jnp.float32
    return pl.pallas_call(
        functools.partial(kernel, img_count, blk_count),
        out_shape=(
            jax.ShapeDtypeStruct((local, tiles, block, block), full),
            jax.ShapeDtypeStruct((local, block), full),
            jax.ShapeDtypeStruct((local, block), full),
        ),
        in_specs=[vmem, smem, smem, smem, vmem, vmem, vmem, vmem, vmem, smem],
        out_specs=(vmem, vmem, vmem),
        scratch_shapes=[
            pltpu.VMEM((near, block, width), half),
            pltpu.VMEM((near, block, width), half),
            pltpu.VMEM((near, block, width), half),
            pltpu.VMEM((near, block, width), half),
            pltpu.VMEM((local, block, width), half),
            pltpu.VMEM((local, block, merge_weight.shape[1]), full),
            pltpu.VMEM((local, tiles, block, block), full),
            pltpu.VMEM((ITERS, 3, group, block), full),
            pltpu.VMEM((ITERS, 5, blk_count, 3, group, block), full),
            pltpu.VMEM((near, block), full),
            dma((3, blk_count)),
            dma((3, blk_count)),
            dma((3, blk_count)),
            dma((3, blk_count)),
            dma((ITERS, 5, blk_count)),
            dma((ITERS, 5, blk_count)),
        ],
        compiler_params=pltpu.CompilerParams(collective_id=0, has_side_effects=True),
    )(
        descriptors,
        covisible,
        tile_counts,
        keypoints,
        query_weight,
        key_weight,
        value_weight,
        merge_weight,
        output_weight,
        dustbin,
    )


def solution(mesh):
    in_specs = (
        P(("img", "blk"), None, None),
        P(("img", "blk"), None),
        P(("img", "blk")),
        P(),
        P(),
        P(),
        P(),
        P(),
        P(),
        P(),
    )
    out_specs = (
        P(("img", "blk"), None, None, None),
        P(("img", "blk"), None),
        P(("img", "blk"), None),
    )
    return jax.shard_map(
        functools.partial(on_device, mesh.shape["img"], mesh.shape["blk"]),
        mesh=mesh,
        in_specs=in_specs,
        out_specs=out_specs,
        check_vma=False,
    )
```

```python
import functools
import math

import jax
import jax.numpy as jnp
from jax import lax
from jax.experimental import pallas as pl
from jax.experimental.pallas import tpu as pltpu
from jax.sharding import PartitionSpec as P

HEADS = 4
ITERS = 3
DEAD = -1e30
MESH = pl.DeviceIdType.MESH


def kernel(
    img_count,
    blk_count,
    desc_in,
    cov_in,
    count_in,
    kpt_in,
    wq_in,
    wk_in,
    wv_in,
    wm_in,
    wo_in,
    dust_in,
    plan_ref,
    row_ref,
    col_ref,
    desc_ref,
    cov_ref,
    count_ref,
    kpt_ref,
    wq_ref,
    wk_ref,
    wv_ref,
    wm_ref,
    wo_ref,
    dust_ref,
    load_sem,
    near_desc,
    near_ref,
    near_k,
    near_v,
    query,
    merged,
    scores,
    acc,
    mass_in,
    pot,
    desc_ssem,
    desc_rsem,
    ref_ssem,
    ref_rsem,
    mass_ssem,
    mass_rsem,
):
    local, block, width = desc_ref.shape
    tiles = cov_ref.shape[1]
    group = local * blk_count
    head_dim = width // HEADS
    img = lax.axis_index("img")
    blk = lax.axis_index("blk")
    others = [lax.rem(blk + step, blk_count) for step in range(1, blk_count)]
    first_block = (img - 1) * group

    def exists(shift):
        if shift == 0:
            return True
        return img + shift < img_count if shift > 0 else img + shift >= 0

    def guarded(shift, body):
        if shift == 0:
            body()
        else:
            pl.when(exists(shift))(body)

    pairs = (
        (desc_in, desc_ref),
        (wq_in, wq_ref),
        (wk_in, wk_ref),
        (wv_in, wv_ref),
        (wm_in, wm_ref),
        (cov_in, cov_ref),
        (count_in, count_ref),
        (kpt_in, kpt_ref),
        (dust_in, dust_ref),
        (wo_in, wo_ref),
    )
    loads = [
        pltpu.make_async_copy(source, target, load_sem.at[place])
        for place, (source, target) in enumerate(pairs)
    ]

    barrier = pltpu.get_barrier_semaphore()
    for shift in range(-2, 3):
        def greet(shift=shift):
            for member in others if shift == 0 else range(blk_count):
                pl.semaphore_signal(
                    barrier, inc=1, device_id=(img + shift, member), device_id_type=MESH
                )
        guarded(shift, greet)

    for load in loads:
        load.start()

    def slot(near, section, member):
        return near.at[pl.ds((section * blk_count + member) * local, local)]

    def sender(source, near, ssem, rsem, section, shift, member):
        return pltpu.make_async_remote_copy(
            src_ref=source,
            dst_ref=slot(near, section, blk),
            send_sem=ssem.at[section, member],
            recv_sem=rsem.at[section, blk],
            device_id=(img + shift, member),
            device_id_type=MESH,
        )

    def arrival(near, ssem, rsem, section, member):
        here = slot(near, section, member)
        return pltpu.make_async_remote_copy(
            src_ref=here,
            dst_ref=here,
            send_sem=ssem.at[section, member],
            recv_sem=rsem.at[section, member],
            device_id=(img, others[0]),
            device_id_type=MESH,
        )

    def send_own(source, near, ssem, rsem):
        for shift in (1, -1):
            guarded(
                shift,
                lambda shift=shift: sender(
                    source, near, ssem, rsem, 1 - shift, shift, blk
                ).start(),
            )
        for member in others:
            sender(source, near, ssem, rsem, 1, 0, member).start()

    def relay(near, ssem, rsem, section):
        def body():
            arrival(near, ssem, rsem, section, blk).wait_recv()
            for member in others:
                sender(slot(near, section, blk), near, ssem, rsem, section, 0, member).start()
        guarded(section - 1, body)

    def wait_relayed(near, ssem, rsem, section, after=None):
        def body():
            for member in others:
                arrival(near, ssem, rsem, section, member).wait_recv()
                if after is not None:
                    after(section, member)
        guarded(section - 1, body)

    def drain(source, near, ssem, rsem):
        for shift in (1, -1):
            guarded(
                shift,
                lambda shift=shift: sender(
                    source, near, ssem, rsem, 1 - shift, shift, blk
                ).wait_send(),
            )
        for section in range(3):
            def body(section=section):
                for member in others:
                    sender(source, near, ssem, rsem, section, 0, member).wait_send()
            guarded(section - 1, body)

    def project(rows, section, member):
        where_to = pl.ds((section * blk_count + member) * local, local)
        for weight, target in ((wk_ref, near_k), (wv_ref, near_v)):
            out = jnp.dot(rows, weight[...], preferred_element_type=jnp.float32)
            target[where_to] = out.astype(jnp.bfloat16).reshape(local, block, width)

    def project_near(section, member):
        rows = near_desc[pl.ds((section * blk_count + member) * local, local)]
        project(rows.reshape(local * block, width), section, member)

    for source in range(-2, 3):
        if source != 0:
            @pl.when(jnp.logical_not(exists(source)))
            def _(source=source):
                for sweep in range(ITERS):
                    mass_in[sweep, source + 2] = jnp.zeros(mass_in.shape[2:], jnp.float32)

    low = jnp.maximum(img - 2, 0)
    high = jnp.minimum(img + 2, img_count - 1)
    pl.semaphore_wait(barrier, (high - low + 1) * blk_count - 1)
    send_own(desc_in, near_desc, desc_ssem, desc_rsem)
    for load in loads:
        load.wait()
    own = desc_ref[...].reshape(local * block, width)

    scaled = jnp.dot(own, wq_ref[...], preferred_element_type=jnp.float32) * (
        1.0 / math.sqrt(head_dim)
    )
    query[...] = scaled.astype(jnp.bfloat16).reshape(local, block, width)
    project(own, 1, blk)
    merged[...] = jnp.dot(
        own, wm_ref[pl.ds(0, width), :], preferred_element_type=jnp.float32
    ).reshape(merged.shape)
    wait_relayed(near_desc, desc_ssem, desc_rsem, 1, project_near)
    for section in (0, 2):
        relay(near_desc, desc_ssem, desc_rsem, section)
    for section in (0, 2):
        guarded(section - 1, lambda section=section: project_near(section, blk))
    for section in (0, 2):
        wait_relayed(near_desc, desc_ssem, desc_rsem, section, project_near)

    lanes = lax.broadcasted_iota(jnp.int32, (1, block), 1)
    rows_at = lax.broadcasted_iota(jnp.int32, (block, 1), 0)
    head_of = lax.broadcasted_iota(jnp.int32, (1, width), 1) // head_dim
    heads = [head_of == head for head in range(HEADS)]
    own_kpt = [kpt_ref[(img * blk_count + blk) * local + r] for r in range(local)]
    near_ids = [
        [jnp.clip(cov_ref[r, t] - first_block, 0, 3 * group - 1) for t in range(tiles)]
        for r in range(local)
    ]
    limits = [
        [
            jnp.where(t < count_ref[r], kpt_ref[jnp.clip(cov_ref[r, t], 0, kpt_ref.shape[0] - 1)], 0)
            for t in range(tiles)
        ]
        for r in range(local)
    ]
    biases = [
        [jnp.where(lanes < limits[r][t], 0.0, DEAD) for t in range(tiles)] for r in range(local)
    ]

    for r in range(local):
        keys = jnp.concatenate([near_k[near_ids[r][t]] for t in range(tiles)], axis=0)
        values = jnp.concatenate([near_v[near_ids[r][t]] for t in range(tiles)], axis=0)
        q = query[r]
        bias = jnp.concatenate(biases[r], axis=1)
        message = jnp.zeros((block, width), jnp.float32)
        for head in range(HEADS):
            logits = lax.dot_general(
                jnp.where(heads[head], q, jnp.zeros_like(q)),
                keys,
                (((1,), (1,)), ((), ())),
                preferred_element_type=jnp.float32,
            ) + bias
            weights = jnp.exp(logits - jnp.max(logits, axis=1, keepdims=True))
            weights = weights * (1.0 / jnp.sum(weights, axis=1, keepdims=True))
            out = jnp.dot(
                weights.astype(jnp.bfloat16), values, preferred_element_type=jnp.float32
            )
            message = jnp.where(heads[head], out, message)
        hidden = jnp.maximum(
            merged[r]
            + jnp.dot(
                message.astype(jnp.bfloat16),
                wm_ref[pl.ds(width, width), :],
                preferred_element_type=jnp.float32,
            ),
            0.0,
        ).astype(jnp.bfloat16)
        refined = desc_ref[r].astype(jnp.float32) + jnp.dot(
            hidden, wo_ref[...], preferred_element_type=jnp.float32
        )
        near_ref[group + blk * local + r] = refined.astype(jnp.bfloat16)

    own_slot = slot(near_ref, 1, blk)
    send_own(own_slot, near_ref, ref_ssem, ref_rsem)
    drain(desc_in, near_desc, desc_ssem, desc_rsem)
    for section in (0, 2):
        relay(near_ref, ref_ssem, ref_rsem, section)
    for section in (1, 0, 2):
        wait_relayed(near_ref, ref_ssem, ref_rsem, section)

    dust = dust_ref[0]
    row_live = [rows_at < own_kpt[r] for r in range(local)]
    for r in range(local):
        mine = near_ref[group + blk * local + r] * jnp.asarray(
            1.0 / math.sqrt(width), jnp.bfloat16
        )
        row_bias = jnp.where(row_live[r], 0.0, DEAD)
        for t in range(tiles):
            out = lax.dot_general(
                mine,
                near_ref[near_ids[r][t]],
                (((1,), (1,)), ((), ())),
                preferred_element_type=jnp.float32,
            )
            scores[r, t] = out + (row_bias + biases[r][t])

    slots = lax.broadcasted_iota(jnp.int32, (group, 1), 0)
    pots = [jnp.zeros((group, block), jnp.float32)] * 3

    def mass_copy(sweep, shift, member):
        first, count = max(0, shift), 3 - abs(shift)
        return pltpu.make_async_remote_copy(
            src_ref=acc.at[sweep, pl.ds(first, count)],
            dst_ref=mass_in.at[sweep, 2 - shift, blk, pl.ds(first, count)],
            send_sem=mass_ssem.at[sweep, shift + 2, member],
            recv_sem=mass_rsem.at[sweep, 2 - shift, blk],
            device_id=(img + shift, member),
            device_id_type=MESH,
        )

    def mass_arrival(sweep, source, member):
        first, count = max(0, -source), 3 - abs(source)
        here = mass_in.at[sweep, source + 2, member, pl.ds(first, count)]
        return pltpu.make_async_remote_copy(
            src_ref=here,
            dst_ref=here,
            send_sem=mass_ssem.at[sweep, source + 2, member],
            recv_sem=mass_rsem.at[sweep, source + 2, member],
            device_id=(img, others[0]),
            device_id_type=MESH,
        )

    def each_partner(body):
        for shift in (-1, 1, -2, 2, 0):
            def run(shift=shift):
                for member in others if shift == 0 else range(blk_count):
                    body(shift, member)
            guarded(shift, run)

    row_pots = [None] * local
    for sweep in range(ITERS):
        spread = [jnp.zeros((group, block), jnp.float32)] * 3
        for r in range(local):
            def shifted(t):
                if sweep == 0:
                    return scores[r, t]
                return scores[r, t] + pot[pl.ds(near_ids[r][t], 1), :]
            top = shifted(0)
            for t in range(1, tiles):
                top = jnp.maximum(top, shifted(t))
            top = jnp.maximum(jnp.max(top, axis=1, keepdims=True), dust)
            terms = [jnp.exp(shifted(t) - top) for t in range(tiles)]
            total = functools.reduce(jnp.add, terms)
            total = jnp.sum(total, axis=1, keepdims=True) + jnp.exp(dust - top)
            row_pots[r] = -(top + jnp.log(total))
            inverse = 1.0 / total
            for t in range(tiles):
                mass = jnp.sum(terms[t] * inverse, axis=0, keepdims=True)
                for section in range(3):
                    hit = slots == near_ids[r][t] - section * group
                    spread[section] = spread[section] + jnp.where(hit, mass, 0.0)
        for section in range(3):
            acc[sweep, section] = spread[section]
        each_partner(lambda shift, member: mass_copy(sweep, shift, member).start())
        if sweep == 0:
            drain(own_slot, near_ref, ref_ssem, ref_rsem)
        if sweep == ITERS - 1:
            for r in range(local):
                row = jnp.broadcast_to(row_pots[r], (block, block))
                row = jnp.sum(jnp.where(rows_at == lanes, row, 0.0), axis=0, keepdims=True)
                row_ref[pl.ds(r, 1), :] = jnp.where(lanes < own_kpt[r], dust + row, 0.0)
                for t in range(tiles):
                    scores[r, t] = scores[r, t] + row_pots[r]
        sums = list(spread)
        each_partner(lambda source, member: mass_arrival(sweep, source, member).wait_recv())
        for source in range(-2, 3):
            for member in others if source == 0 else range(blk_count):
                for section in range(3):
                    if 0 <= section - source <= 2:
                        sums[section] = sums[section] + mass_in[
                            sweep, source + 2, member, section - source
                        ]
        for section in range(3):
            pots[section] = pots[section] - jnp.log(
                sums[section] + jnp.exp(dust + pots[section])
            )
            pot[pl.ds(section * group, group), :] = pots[section]

    for r in range(local):
        for t in range(tiles):
            out = scores[r, t] + pot[pl.ds(near_ids[r][t], 1), :]
            valid = jnp.where(row_live[r], lanes, block) < limits[r][t]
            plan_ref[r, t] = jnp.where(valid, out, 0.0)
        mine = pot[pl.ds(group + blk * local + r, 1), :]
        col_ref[pl.ds(r, 1), :] = jnp.where(lanes < own_kpt[r], dust + mine, 0.0)
    for sweep in range(ITERS):
        each_partner(lambda shift, member: mass_copy(sweep, shift, member).wait_send())


def on_device(
    img_count,
    blk_count,
    descriptors,
    covisible,
    tile_counts,
    keypoints,
    query_weight,
    key_weight,
    value_weight,
    merge_weight,
    output_weight,
    dustbin,
):
    local, block, width = descriptors.shape
    tiles = covisible.shape[1]
    group = local * blk_count
    near = 3 * group
    vmem = pl.BlockSpec(memory_space=pltpu.VMEM)
    hbm = pl.BlockSpec(memory_space=pltpu.HBM)
    dma = pltpu.SemaphoreType.DMA
    half = jnp.bfloat16
    full = jnp.float32
    return pl.pallas_call(
        functools.partial(kernel, img_count, blk_count),
        out_shape=(
            jax.ShapeDtypeStruct((local, tiles, block, block), full),
            jax.ShapeDtypeStruct((local, block), full),
            jax.ShapeDtypeStruct((local, block), full),
        ),
        in_specs=[hbm] * 10,
        out_specs=(vmem, vmem, vmem),
        scratch_shapes=[
            pltpu.VMEM(descriptors.shape, half),
            pltpu.SMEM(covisible.shape, jnp.int32),
            pltpu.SMEM(tile_counts.shape, jnp.int32),
            pltpu.SMEM(keypoints.shape, jnp.int32),
            pltpu.VMEM(query_weight.shape, half),
            pltpu.VMEM(key_weight.shape, half),
            pltpu.VMEM(value_weight.shape, half),
            pltpu.VMEM(merge_weight.shape, half),
            pltpu.VMEM(output_weight.shape, half),
            pltpu.SMEM(dustbin.shape, full),
            dma((10,)),
            pltpu.VMEM((near, block, width), half),
            pltpu.VMEM((near, block, width), half),
            pltpu.VMEM((near, block, width), half),
            pltpu.VMEM((near, block, width), half),
            pltpu.VMEM((local, block, width), half),
            pltpu.VMEM((local, block, merge_weight.shape[1]), full),
            pltpu.VMEM((local, tiles, block, block), full),
            pltpu.VMEM((ITERS, 3, group, block), full),
            pltpu.VMEM((ITERS, 5, blk_count, 3, group, block), full),
            pltpu.VMEM((near, block), full),
            dma((3, blk_count)),
            dma((3, blk_count)),
            dma((3, blk_count)),
            dma((3, blk_count)),
            dma((ITERS, 5, blk_count)),
            dma((ITERS, 5, blk_count)),
        ],
        compiler_params=pltpu.CompilerParams(
            collective_id=0, has_side_effects=True
        ),
    )(
        descriptors,
        covisible,
        tile_counts,
        keypoints,
        query_weight,
        key_weight,
        value_weight,
        merge_weight,
        output_weight,
        dustbin,
    )


def solution(mesh):
    in_specs = (
        P(("img", "blk"), None, None),
        P(("img", "blk"), None),
        P(("img", "blk")),
        P(),
        P(),
        P(),
        P(),
        P(),
        P(),
        P(),
    )
    out_specs = (
        P(("img", "blk"), None, None, None),
        P(("img", "blk"), None),
        P(("img", "blk"), None),
    )
    return jax.shard_map(
        functools.partial(on_device, mesh.shape["img"], mesh.shape["blk"]),
        mesh=mesh,
        in_specs=in_specs,
        out_specs=out_specs,
        check_vma=False,
    )
```

```python
import functools
import math

import jax
import jax.numpy as jnp
from jax import lax
from jax.experimental import pallas as pl
from jax.experimental.pallas import tpu as pltpu
from jax.sharding import PartitionSpec as P

HEADS = 4
ITERS = 3
DEAD = -1e30
MESH = pl.DeviceIdType.MESH


def kernel(
    img_count,
    blk_count,
    desc_in,
    cov_in,
    count_in,
    kpt_in,
    wq_in,
    wk_in,
    wv_in,
    wm_in,
    wo_in,
    dust_in,
    base_out,
    tail_ref,
    desc_ref,
    cov_ref,
    count_ref,
    kpt_ref,
    wq_ref,
    wk_ref,
    wv_ref,
    wm_ref,
    wo_ref,
    dust_ref,
    load_sem,
    base_sem,
    near_desc,
    near_ref,
    near_k,
    near_v,
    query,
    merged,
    scores,
    acc,
    mass_in,
    pot,
    desc_ssem,
    desc_rsem,
    ref_ssem,
    ref_rsem,
    mass_ssem,
    mass_rsem,
):
    local, block, width = desc_ref.shape
    tiles = cov_ref.shape[1]
    group = local * blk_count
    head_dim = width // HEADS
    img = lax.axis_index("img")
    blk = lax.axis_index("blk")
    others = [lax.rem(blk + step, blk_count) for step in range(1, blk_count)]
    first_block = (img - 1) * group

    def exists(shift):
        if shift == 0:
            return True
        return img + shift < img_count if shift > 0 else img + shift >= 0

    def guarded(shift, body):
        if shift == 0:
            body()
        else:
            pl.when(exists(shift))(body)

    pairs = (
        (desc_in, desc_ref),
        (wq_in, wq_ref),
        (wk_in, wk_ref),
        (wv_in, wv_ref),
        (wm_in, wm_ref),
        (cov_in, cov_ref),
        (count_in, count_ref),
        (kpt_in, kpt_ref),
        (dust_in, dust_ref),
        (wo_in, wo_ref),
    )
    loads = [
        pltpu.make_async_copy(source, target, load_sem.at[place])
        for place, (source, target) in enumerate(pairs)
    ]

    barrier = pltpu.get_barrier_semaphore()
    for shift in range(-2, 3):
        def greet(shift=shift):
            for member in others if shift == 0 else range(blk_count):
                pl.semaphore_signal(
                    barrier, inc=1, device_id=(img + shift, member), device_id_type=MESH
                )
        guarded(shift, greet)

    for load in loads:
        load.start()

    def slot(near, section, member):
        return near.at[pl.ds((section * blk_count + member) * local, local)]

    def sender(source, near, ssem, rsem, section, shift, member):
        return pltpu.make_async_remote_copy(
            src_ref=source,
            dst_ref=slot(near, section, blk),
            send_sem=ssem.at[section, member],
            recv_sem=rsem.at[section, blk],
            device_id=(img + shift, member),
            device_id_type=MESH,
        )

    def arrival(near, ssem, rsem, section, member):
        here = slot(near, section, member)
        return pltpu.make_async_remote_copy(
            src_ref=here,
            dst_ref=here,
            send_sem=ssem.at[section, member],
            recv_sem=rsem.at[section, member],
            device_id=(img, others[0]),
            device_id_type=MESH,
        )

    def send_own(source, near, ssem, rsem):
        for shift in (1, -1):
            guarded(
                shift,
                lambda shift=shift: sender(
                    source, near, ssem, rsem, 1 - shift, shift, blk
                ).start(),
            )
        for member in others:
            sender(source, near, ssem, rsem, 1, 0, member).start()

    def relay(near, ssem, rsem, section):
        def body():
            arrival(near, ssem, rsem, section, blk).wait_recv()
            for member in others:
                sender(slot(near, section, blk), near, ssem, rsem, section, 0, member).start()
        guarded(section - 1, body)

    def wait_relayed(near, ssem, rsem, section, after=None):
        def body():
            for member in others:
                arrival(near, ssem, rsem, section, member).wait_recv()
                if after is not None:
                    after(section, member)
        guarded(section - 1, body)

    def drain(source, near, ssem, rsem):
        for shift in (1, -1):
            guarded(
                shift,
                lambda shift=shift: sender(
                    source, near, ssem, rsem, 1 - shift, shift, blk
                ).wait_send(),
            )
        for section in range(3):
            def body(section=section):
                for member in others:
                    sender(source, near, ssem, rsem, section, 0, member).wait_send()
            guarded(section - 1, body)

    def project(rows, section, member):
        where_to = pl.ds((section * blk_count + member) * local, local)
        for weight, target in ((wk_ref, near_k), (wv_ref, near_v)):
            out = jnp.dot(rows, weight[...], preferred_element_type=jnp.float32)
            target[where_to] = out.astype(jnp.bfloat16).reshape(local, block, width)

    def project_near(section, member):
        rows = near_desc[pl.ds((section * blk_count + member) * local, local)]
        project(rows.reshape(local * block, width), section, member)

    for source in range(-2, 3):
        if source != 0:
            @pl.when(jnp.logical_not(exists(source)))
            def _(source=source):
                for sweep in range(ITERS):
                    mass_in[sweep, source + 2] = jnp.zeros(mass_in.shape[2:], jnp.float32)

    low = jnp.maximum(img - 2, 0)
    high = jnp.minimum(img + 2, img_count - 1)
    pl.semaphore_wait(barrier, (high - low + 1) * blk_count - 1)
    send_own(desc_in, near_desc, desc_ssem, desc_rsem)
    for load in loads:
        load.wait()
    own = desc_ref[...].reshape(local * block, width)

    scaled = jnp.dot(own, wq_ref[...], preferred_element_type=jnp.float32) * (
        1.0 / math.sqrt(head_dim)
    )
    query[...] = scaled.astype(jnp.bfloat16).reshape(local, block, width)
    project(own, 1, blk)
    merged[...] = jnp.dot(
        own, wm_ref[pl.ds(0, width), :], preferred_element_type=jnp.float32
    ).reshape(merged.shape)
    wait_relayed(near_desc, desc_ssem, desc_rsem, 1, project_near)
    for section in (0, 2):
        relay(near_desc, desc_ssem, desc_rsem, section)
    for section in (0, 2):
        guarded(section - 1, lambda section=section: project_near(section, blk))
    for section in (0, 2):
        wait_relayed(near_desc, desc_ssem, desc_rsem, section, project_near)

    lanes = lax.broadcasted_iota(jnp.int32, (1, block), 1)
    rows_at = lax.broadcasted_iota(jnp.int32, (block, 1), 0)
    head_of = lax.broadcasted_iota(jnp.int32, (1, width), 1) // head_dim
    heads = [head_of == head for head in range(HEADS)]
    own_kpt = [kpt_ref[(img * blk_count + blk) * local + r] for r in range(local)]
    near_ids = [
        [jnp.clip(cov_ref[r, t] - first_block, 0, 3 * group - 1) for t in range(tiles)]
        for r in range(local)
    ]
    limits = [
        [
            jnp.where(t < count_ref[r], kpt_ref[jnp.clip(cov_ref[r, t], 0, kpt_ref.shape[0] - 1)], 0)
            for t in range(tiles)
        ]
        for r in range(local)
    ]
    biases = [
        [jnp.where(lanes < limits[r][t], 0.0, DEAD) for t in range(tiles)] for r in range(local)
    ]

    for r in range(local):
        keys = jnp.concatenate([near_k[near_ids[r][t]] for t in range(tiles)], axis=0)
        values = jnp.concatenate([near_v[near_ids[r][t]] for t in range(tiles)], axis=0)
        q = query[r]
        bias = jnp.concatenate(biases[r], axis=1)
        message = jnp.zeros((block, width), jnp.float32)
        for head in range(HEADS):
            logits = lax.dot_general(
                jnp.where(heads[head], q, jnp.zeros_like(q)),
                keys,
                (((1,), (1,)), ((), ())),
                preferred_element_type=jnp.float32,
            ) + bias
            weights = jnp.exp(logits - jnp.max(logits, axis=1, keepdims=True))
            weights = weights * (1.0 / jnp.sum(weights, axis=1, keepdims=True))
            out = jnp.dot(
                weights.astype(jnp.bfloat16), values, preferred_element_type=jnp.float32
            )
            message = jnp.where(heads[head], out, message)
        hidden = jnp.maximum(
            merged[r]
            + jnp.dot(
                message.astype(jnp.bfloat16),
                wm_ref[pl.ds(width, width), :],
                preferred_element_type=jnp.float32,
            ),
            0.0,
        ).astype(jnp.bfloat16)
        refined = desc_ref[r].astype(jnp.float32) + jnp.dot(
            hidden, wo_ref[...], preferred_element_type=jnp.float32
        )
        near_ref[group + blk * local + r] = refined.astype(jnp.bfloat16)

    own_slot = slot(near_ref, 1, blk)
    send_own(own_slot, near_ref, ref_ssem, ref_rsem)
    drain(desc_in, near_desc, desc_ssem, desc_rsem)
    for section in (0, 2):
        relay(near_ref, ref_ssem, ref_rsem, section)
    for section in (1, 0, 2):
        wait_relayed(near_ref, ref_ssem, ref_rsem, section)

    dust = dust_ref[0]
    row_live = [rows_at < own_kpt[r] for r in range(local)]
    for r in range(local):
        mine = near_ref[group + blk * local + r] * jnp.asarray(
            1.0 / math.sqrt(width), jnp.bfloat16
        )
        row_bias = jnp.where(row_live[r], 0.0, DEAD)
        for t in range(tiles):
            out = lax.dot_general(
                mine,
                near_ref[near_ids[r][t]],
                (((1,), (1,)), ((), ())),
                preferred_element_type=jnp.float32,
            )
            scores[r, t] = out + (row_bias + biases[r][t])

    slots = lax.broadcasted_iota(jnp.int32, (group, 1), 0)
    pots = [jnp.zeros((group, block), jnp.float32)] * 3

    def mass_copy(sweep, shift, member):
        first, count = max(0, shift), 3 - abs(shift)
        return pltpu.make_async_remote_copy(
            src_ref=acc.at[sweep, pl.ds(first, count)],
            dst_ref=mass_in.at[sweep, 2 - shift, blk, pl.ds(first, count)],
            send_sem=mass_ssem.at[sweep, shift + 2, member],
            recv_sem=mass_rsem.at[sweep, 2 - shift, blk],
            device_id=(img + shift, member),
            device_id_type=MESH,
        )

    def mass_arrival(sweep, source, member):
        first, count = max(0, -source), 3 - abs(source)
        here = mass_in.at[sweep, source + 2, member, pl.ds(first, count)]
        return pltpu.make_async_remote_copy(
            src_ref=here,
            dst_ref=here,
            send_sem=mass_ssem.at[sweep, source + 2, member],
            recv_sem=mass_rsem.at[sweep, source + 2, member],
            device_id=(img, others[0]),
            device_id_type=MESH,
        )

    def each_partner(body):
        for shift in (-1, 1, -2, 2, 0):
            def run(shift=shift):
                for member in others if shift == 0 else range(blk_count):
                    body(shift, member)
            guarded(shift, run)

    def base_copy(r, t):
        return pltpu.make_async_copy(scores.at[r, t], base_out.at[r, t], base_sem.at[r, t])

    row_pots = [None] * local
    for sweep in range(ITERS):
        spread = [jnp.zeros((group, block), jnp.float32)] * 3
        for r in range(local):
            def shifted(t):
                if sweep == 0:
                    return scores[r, t]
                return scores[r, t] + pot[pl.ds(near_ids[r][t], 1), :]
            top = shifted(0)
            for t in range(1, tiles):
                top = jnp.maximum(top, shifted(t))
            top = jnp.maximum(jnp.max(top, axis=1, keepdims=True), dust)
            terms = [jnp.exp(shifted(t) - top) for t in range(tiles)]
            total = functools.reduce(jnp.add, terms)
            total = jnp.sum(total, axis=1, keepdims=True) + jnp.exp(dust - top)
            row_pots[r] = -(top + jnp.log(total))
            inverse = 1.0 / total
            for t in range(tiles):
                mass = jnp.sum(terms[t] * inverse, axis=0, keepdims=True)
                for section in range(3):
                    hit = slots == near_ids[r][t] - section * group
                    spread[section] = spread[section] + jnp.where(hit, mass, 0.0)
        for section in range(3):
            acc[sweep, section] = spread[section]
        each_partner(lambda shift, member: mass_copy(sweep, shift, member).start())
        if sweep == 0:
            drain(own_slot, near_ref, ref_ssem, ref_rsem)
        if sweep == ITERS - 1:
            for r in range(local):
                row = jnp.broadcast_to(row_pots[r], (block, block))
                row = jnp.sum(jnp.where(rows_at == lanes, row, 0.0), axis=0, keepdims=True)
                tail_ref[pl.ds(local * tiles + r, 1), :] = jnp.where(lanes < own_kpt[r], dust + row, 0.0)
                for t in range(tiles):
                    scores[r, t] = scores[r, t] + row_pots[r]
                    base_copy(r, t).start()
        sums = list(spread)
        each_partner(lambda source, member: mass_arrival(sweep, source, member).wait_recv())
        for source in range(-2, 3):
            for member in others if source == 0 else range(blk_count):
                for section in range(3):
                    if 0 <= section - source <= 2:
                        sums[section] = sums[section] + mass_in[
                            sweep, source + 2, member, section - source
                        ]
        for section in range(3):
            pots[section] = pots[section] - jnp.log(
                sums[section] + jnp.exp(dust + pots[section])
            )
            pot[pl.ds(section * group, group), :] = pots[section]

    for r in range(local):
        for t in range(tiles):
            tail_ref[pl.ds(r * tiles + t, 1), :] = pot[pl.ds(near_ids[r][t], 1), :]
        mine = pot[pl.ds(group + blk * local + r, 1), :]
        tail_ref[pl.ds(local * (tiles + 1) + r, 1), :] = jnp.where(lanes < own_kpt[r], dust + mine, 0.0)
    for sweep in range(ITERS):
        each_partner(lambda shift, member: mass_copy(sweep, shift, member).wait_send())
    for r in range(local):
        for t in range(tiles):
            base_copy(r, t).wait()


def finish(
    base_in, tail_in, plan_out, row_out, col_out, tail_ref, taken, made, in_sem, out_sem, end_sem
):
    local, tiles = base_in.shape[:2]
    places = [(r, t) for r in range(local) for t in range(tiles)]

    def fetch(r, t):
        return pltpu.make_async_copy(base_in.at[r, t], taken.at[r, t], in_sem.at[r, t])

    def put(r, t):
        return pltpu.make_async_copy(made.at[r, t], plan_out.at[r, t], out_sem.at[r, t])

    head = pltpu.make_async_copy(tail_in, tail_ref, end_sem.at[0])
    head.start()
    for place in places:
        fetch(*place).start()
    head.wait()
    ends = [
        pltpu.make_async_copy(
            tail_ref.at[pl.ds(local * (tiles + step), local)], target, end_sem.at[1 + step]
        )
        for step, target in enumerate((row_out, col_out))
    ]
    for end in ends:
        end.start()
    for r, t in places:
        fetch(r, t).wait()
        base = taken[r, t]
        out = base + tail_ref[pl.ds(r * tiles + t, 1), :]
        made[r, t] = jnp.where(base > 0.1 * DEAD, out, 0.0)
        put(r, t).start()
    for place in places:
        put(*place).wait()
    for end in ends:
        end.wait()


def on_device(
    img_count,
    blk_count,
    descriptors,
    covisible,
    tile_counts,
    keypoints,
    query_weight,
    key_weight,
    value_weight,
    merge_weight,
    output_weight,
    dustbin,
):
    local, block, width = descriptors.shape
    tiles = covisible.shape[1]
    group = local * blk_count
    near = 3 * group
    vmem = pl.BlockSpec(memory_space=pltpu.VMEM)
    hbm = pl.BlockSpec(memory_space=pltpu.HBM)
    dma = pltpu.SemaphoreType.DMA
    half = jnp.bfloat16
    full = jnp.float32
    base, tail = pl.pallas_call(
        functools.partial(kernel, img_count, blk_count),
        out_shape=(
            jax.ShapeDtypeStruct((local, tiles, block, block), full),
            jax.ShapeDtypeStruct((local * (tiles + 2), block), full),
        ),
        in_specs=[hbm] * 10,
        out_specs=(hbm, vmem),
        scratch_shapes=[
            pltpu.VMEM(descriptors.shape, half),
            pltpu.SMEM(covisible.shape, jnp.int32),
            pltpu.SMEM(tile_counts.shape, jnp.int32),
            pltpu.SMEM(keypoints.shape, jnp.int32),
            pltpu.VMEM(query_weight.shape, half),
            pltpu.VMEM(key_weight.shape, half),
            pltpu.VMEM(value_weight.shape, half),
            pltpu.VMEM(merge_weight.shape, half),
            pltpu.VMEM(output_weight.shape, half),
            pltpu.SMEM(dustbin.shape, full),
            dma((10,)),
            dma((descriptors.shape[0], tiles)),
            pltpu.VMEM((near, block, width), half),
            pltpu.VMEM((near, block, width), half),
            pltpu.VMEM((near, block, width), half),
            pltpu.VMEM((near, block, width), half),
            pltpu.VMEM((local, block, width), half),
            pltpu.VMEM((local, block, merge_weight.shape[1]), full),
            pltpu.VMEM((local, tiles, block, block), full),
            pltpu.VMEM((ITERS, 3, group, block), full),
            pltpu.VMEM((ITERS, 5, blk_count, 3, group, block), full),
            pltpu.VMEM((near, block), full),
            dma((3, blk_count)),
            dma((3, blk_count)),
            dma((3, blk_count)),
            dma((3, blk_count)),
            dma((ITERS, 5, blk_count)),
            dma((ITERS, 5, blk_count)),
        ],
        compiler_params=pltpu.CompilerParams(
            collective_id=0, has_side_effects=True
        ),
    )(
        descriptors,
        covisible,
        tile_counts,
        keypoints,
        query_weight,
        key_weight,
        value_weight,
        merge_weight,
        output_weight,
        dustbin,
    )
    return pl.pallas_call(
        finish,
        out_shape=(
            jax.ShapeDtypeStruct(base.shape, full),
            jax.ShapeDtypeStruct((local, block), full),
            jax.ShapeDtypeStruct((local, block), full),
        ),
        in_specs=[hbm, hbm],
        out_specs=(hbm, hbm, hbm),
        scratch_shapes=[
            pltpu.VMEM(tail.shape, full),
            pltpu.VMEM(base.shape, full),
            pltpu.VMEM(base.shape, full),
            dma((local, tiles)),
            dma((local, tiles)),
            dma((3,)),
        ],
    )(base, tail)


def solution(mesh):
    in_specs = (
        P(("img", "blk"), None, None),
        P(("img", "blk"), None),
        P(("img", "blk")),
        P(),
        P(),
        P(),
        P(),
        P(),
        P(),
        P(),
    )
    out_specs = (
        P(("img", "blk"), None, None, None),
        P(("img", "blk"), None),
        P(("img", "blk"), None),
    )
    return jax.shard_map(
        functools.partial(on_device, mesh.shape["img"], mesh.shape["blk"]),
        mesh=mesh,
        in_specs=in_specs,
        out_specs=out_specs,
        check_vma=False,
    )
```

```python
import functools
import math

import jax
import jax.numpy as jnp
from jax import lax
from jax.experimental import pallas as pl
from jax.experimental.pallas import tpu as pltpu
from jax.sharding import PartitionSpec as P

HEADS = 4
ITERS = 3
DEAD = -1e30
MESH = pl.DeviceIdType.MESH


def kernel(
    img_count,
    blk_count,
    desc_in,
    cov_in,
    count_in,
    kpt_in,
    wq_in,
    wk_in,
    wv_in,
    wm_in,
    wo_in,
    dust_in,
    base_out,
    tail_ref,
    desc_ref,
    cov_ref,
    count_ref,
    kpt_ref,
    wq_ref,
    wk_ref,
    wv_ref,
    wm_ref,
    wo_ref,
    dust_ref,
    load_sem,
    base_sem,
    near_desc,
    near_ref,
    near_k,
    near_v,
    query,
    merged,
    scores,
    acc,
    mass_in,
    pot,
    desc_ssem,
    desc_rsem,
    ref_ssem,
    ref_rsem,
    mass_ssem,
    mass_rsem,
):
    local, block, width = desc_ref.shape
    tiles = cov_ref.shape[1]
    group = local * blk_count
    head_dim = width // HEADS
    img = lax.axis_index("img")
    blk = lax.axis_index("blk")
    others = [lax.rem(blk + step, blk_count) for step in range(1, blk_count)]
    first_block = (img - 1) * group

    def exists(shift):
        if shift == 0:
            return True
        return img + shift < img_count if shift > 0 else img + shift >= 0

    def guarded(shift, body):
        if shift == 0:
            body()
        else:
            pl.when(exists(shift))(body)

    pairs = (
        (desc_in, desc_ref),
        (wq_in, wq_ref),
        (wk_in, wk_ref),
        (wv_in, wv_ref),
        (wm_in, wm_ref),
        (cov_in, cov_ref),
        (count_in, count_ref),
        (kpt_in, kpt_ref),
        (dust_in, dust_ref),
        (wo_in, wo_ref),
    )
    loads = [
        pltpu.make_async_copy(source, target, load_sem.at[place])
        for place, (source, target) in enumerate(pairs)
    ]

    barrier = pltpu.get_barrier_semaphore()
    for shift in range(-2, 3):
        def greet(shift=shift):
            for member in others if shift == 0 else range(blk_count):
                pl.semaphore_signal(
                    barrier, inc=1, device_id=(img + shift, member), device_id_type=MESH
                )
        guarded(shift, greet)

    for load in loads:
        load.start()

    def slot(near, section, member):
        return near.at[pl.ds((section * blk_count + member) * local, local)]

    def sender(source, near, ssem, rsem, section, shift, member):
        return pltpu.make_async_remote_copy(
            src_ref=source,
            dst_ref=slot(near, section, blk),
            send_sem=ssem.at[section, member],
            recv_sem=rsem.at[section, blk],
            device_id=(img + shift, member),
            device_id_type=MESH,
        )

    def arrival(near, ssem, rsem, section, member):
        here = slot(near, section, member)
        return pltpu.make_async_remote_copy(
            src_ref=here,
            dst_ref=here,
            send_sem=ssem.at[section, member],
            recv_sem=rsem.at[section, member],
            device_id=(img, others[0]),
            device_id_type=MESH,
        )

    def send_own(source, near, ssem, rsem):
        for shift in (1, -1):
            guarded(
                shift,
                lambda shift=shift: sender(
                    source, near, ssem, rsem, 1 - shift, shift, blk
                ).start(),
            )
        for member in others:
            sender(source, near, ssem, rsem, 1, 0, member).start()

    def relay(near, ssem, rsem, section):
        def body():
            arrival(near, ssem, rsem, section, blk).wait_recv()
            for member in others:
                sender(slot(near, section, blk), near, ssem, rsem, section, 0, member).start()
        guarded(section - 1, body)

    def wait_relayed(near, ssem, rsem, section, after=None):
        def body():
            for member in others:
                arrival(near, ssem, rsem, section, member).wait_recv()
                if after is not None:
                    after(section, member)
        guarded(section - 1, body)

    def drain(source, near, ssem, rsem):
        for shift in (1, -1):
            guarded(
                shift,
                lambda shift=shift: sender(
                    source, near, ssem, rsem, 1 - shift, shift, blk
                ).wait_send(),
            )
        for section in range(3):
            def body(section=section):
                for member in others:
                    sender(source, near, ssem, rsem, section, 0, member).wait_send()
            guarded(section - 1, body)

    def project(rows, section, member):
        where_to = pl.ds((section * blk_count + member) * local, local)
        for weight, target in ((wk_ref, near_k), (wv_ref, near_v)):
            out = jnp.dot(rows, weight[...], preferred_element_type=jnp.float32)
            target[where_to] = out.astype(jnp.bfloat16).reshape(local, block, width)

    def project_near(section, member):
        rows = near_desc[pl.ds((section * blk_count + member) * local, local)]
        project(rows.reshape(local * block, width), section, member)

    for source in range(-2, 3):
        if source != 0:
            @pl.when(jnp.logical_not(exists(source)))
            def _(source=source):
                for sweep in range(ITERS):
                    mass_in[sweep, source + 2] = jnp.zeros(mass_in.shape[2:], jnp.float32)

    low = jnp.maximum(img - 2, 0)
    high = jnp.minimum(img + 2, img_count - 1)
    pl.semaphore_wait(barrier, (high - low + 1) * blk_count - 1)
    send_own(desc_in, near_desc, desc_ssem, desc_rsem)
    for load in loads:
        load.wait()
    own = desc_ref[...].reshape(local * block, width)

    scaled = jnp.dot(own, wq_ref[...], preferred_element_type=jnp.float32) * (
        1.0 / math.sqrt(head_dim)
    )
    query[...] = scaled.astype(jnp.bfloat16).reshape(local, block, width)
    project(own, 1, blk)
    merged[...] = jnp.dot(
        own, wm_ref[pl.ds(0, width), :], preferred_element_type=jnp.float32
    ).reshape(merged.shape)
    wait_relayed(near_desc, desc_ssem, desc_rsem, 1, project_near)
    for section in (0, 2):
        relay(near_desc, desc_ssem, desc_rsem, section)
    for section in (0, 2):
        guarded(section - 1, lambda section=section: project_near(section, blk))
    for section in (0, 2):
        wait_relayed(near_desc, desc_ssem, desc_rsem, section, project_near)

    lanes = lax.broadcasted_iota(jnp.int32, (1, block), 1)
    rows_at = lax.broadcasted_iota(jnp.int32, (block, 1), 0)
    head_of = lax.broadcasted_iota(jnp.int32, (1, width), 1) // head_dim
    heads = [head_of == head for head in range(HEADS)]
    own_kpt = [kpt_ref[(img * blk_count + blk) * local + r] for r in range(local)]
    near_ids = [
        [jnp.clip(cov_ref[r, t] - first_block, 0, 3 * group - 1) for t in range(tiles)]
        for r in range(local)
    ]
    limits = [
        [
            jnp.where(t < count_ref[r], kpt_ref[jnp.clip(cov_ref[r, t], 0, kpt_ref.shape[0] - 1)], 0)
            for t in range(tiles)
        ]
        for r in range(local)
    ]
    biases = [
        [jnp.where(lanes < limits[r][t], 0.0, DEAD) for t in range(tiles)] for r in range(local)
    ]

    for r in range(local):
        keys = jnp.concatenate([near_k[near_ids[r][t]] for t in range(tiles)], axis=0)
        values = jnp.concatenate([near_v[near_ids[r][t]] for t in range(tiles)], axis=0)
        q = query[r]
        bias = jnp.concatenate(biases[r], axis=1)
        spans = [jnp.where(hit, q, jnp.zeros_like(q)) for hit in heads]
        stacked = lax.dot_general(
            jnp.concatenate(spans, axis=0),
            keys,
            (((1,), (1,)), ((), ())),
            preferred_element_type=jnp.float32,
        )
        message = jnp.zeros((block, width), jnp.float32)
        for head in range(HEADS):
            logits = stacked[head * block : (head + 1) * block] + bias
            weights = jnp.exp(logits - jnp.max(logits, axis=1, keepdims=True))
            inverse = 1.0 / jnp.sum(weights, axis=1, keepdims=True)
            out = jnp.dot(
                weights.astype(jnp.bfloat16), values, preferred_element_type=jnp.float32
            )
            message = jnp.where(heads[head], out * inverse, message)
        hidden = jnp.maximum(
            merged[r]
            + jnp.dot(
                message.astype(jnp.bfloat16),
                wm_ref[pl.ds(width, width), :],
                preferred_element_type=jnp.float32,
            ),
            0.0,
        ).astype(jnp.bfloat16)
        refined = desc_ref[r].astype(jnp.float32) + jnp.dot(
            hidden, wo_ref[...], preferred_element_type=jnp.float32
        )
        near_ref[group + blk * local + r] = refined.astype(jnp.bfloat16)

    own_slot = slot(near_ref, 1, blk)
    send_own(own_slot, near_ref, ref_ssem, ref_rsem)
    drain(desc_in, near_desc, desc_ssem, desc_rsem)
    for section in (0, 2):
        relay(near_ref, ref_ssem, ref_rsem, section)
    for section in (1, 0, 2):
        wait_relayed(near_ref, ref_ssem, ref_rsem, section)

    dust = dust_ref[0]
    row_live = [rows_at < own_kpt[r] for r in range(local)]
    for r in range(local):
        mine = near_ref[group + blk * local + r] * jnp.asarray(
            1.0 / math.sqrt(width), jnp.bfloat16
        )
        row_bias = jnp.where(row_live[r], 0.0, DEAD)
        for t in range(tiles):
            out = lax.dot_general(
                mine,
                near_ref[near_ids[r][t]],
                (((1,), (1,)), ((), ())),
                preferred_element_type=jnp.float32,
            )
            scores[r, t] = out + (row_bias + biases[r][t])

    slots = lax.broadcasted_iota(jnp.int32, (group, 1), 0)
    pots = [jnp.zeros((group, block), jnp.float32)] * 3

    def mass_copy(sweep, shift, member):
        first, count = max(0, shift), 3 - abs(shift)
        return pltpu.make_async_remote_copy(
            src_ref=acc.at[sweep, pl.ds(first, count)],
            dst_ref=mass_in.at[sweep, 2 - shift, blk, pl.ds(first, count)],
            send_sem=mass_ssem.at[sweep, shift + 2, member],
            recv_sem=mass_rsem.at[sweep, 2 - shift, blk],
            device_id=(img + shift, member),
            device_id_type=MESH,
        )

    def mass_arrival(sweep, source, member):
        first, count = max(0, -source), 3 - abs(source)
        here = mass_in.at[sweep, source + 2, member, pl.ds(first, count)]
        return pltpu.make_async_remote_copy(
            src_ref=here,
            dst_ref=here,
            send_sem=mass_ssem.at[sweep, source + 2, member],
            recv_sem=mass_rsem.at[sweep, source + 2, member],
            device_id=(img, others[0]),
            device_id_type=MESH,
        )

    def each_partner(body):
        for shift in (-1, 1, -2, 2, 0):
            def run(shift=shift):
                for member in others if shift == 0 else range(blk_count):
                    body(shift, member)
            guarded(shift, run)

    def base_copy(r, t):
        return pltpu.make_async_copy(scores.at[r, t], base_out.at[r, t], base_sem.at[r, t])

    row_pots = [None] * local
    for sweep in range(ITERS):
        spread = [jnp.zeros((group, block), jnp.float32)] * 3
        for r in range(local):
            def shifted(t):
                if sweep == 0:
                    return scores[r, t]
                return scores[r, t] + pot[pl.ds(near_ids[r][t], 1), :]
            top = shifted(0)
            for t in range(1, tiles):
                top = jnp.maximum(top, shifted(t))
            top = jnp.maximum(jnp.max(top, axis=1, keepdims=True), dust)
            terms = [jnp.exp(shifted(t) - top) for t in range(tiles)]
            total = functools.reduce(jnp.add, terms)
            total = jnp.sum(total, axis=1, keepdims=True) + jnp.exp(dust - top)
            row_pots[r] = -(top + jnp.log(total))
            inverse = 1.0 / total
            for t in range(tiles):
                mass = jnp.sum(terms[t] * inverse, axis=0, keepdims=True)
                for section in range(3):
                    hit = slots == near_ids[r][t] - section * group
                    spread[section] = spread[section] + jnp.where(hit, mass, 0.0)
        for section in range(3):
            acc[sweep, section] = spread[section]
        each_partner(lambda shift, member: mass_copy(sweep, shift, member).start())
        if sweep == 0:
            drain(own_slot, near_ref, ref_ssem, ref_rsem)
        if sweep == ITERS - 1:
            for r in range(local):
                row = jnp.broadcast_to(row_pots[r], (block, block))
                row = jnp.sum(jnp.where(rows_at == lanes, row, 0.0), axis=0, keepdims=True)
                tail_ref[pl.ds(local * tiles + r, 1), :] = jnp.where(lanes < own_kpt[r], dust + row, 0.0)
                for t in range(tiles):
                    scores[r, t] = scores[r, t] + row_pots[r]
                    base_copy(r, t).start()
        sums = list(spread)
        each_partner(lambda source, member: mass_arrival(sweep, source, member).wait_recv())
        for source in range(-2, 3):
            for member in others if source == 0 else range(blk_count):
                for section in range(3):
                    if 0 <= section - source <= 2:
                        sums[section] = sums[section] + mass_in[
                            sweep, source + 2, member, section - source
                        ]
        for section in range(3):
            pots[section] = pots[section] - jnp.log(
                sums[section] + jnp.exp(dust + pots[section])
            )
            pot[pl.ds(section * group, group), :] = pots[section]

    for r in range(local):
        for t in range(tiles):
            tail_ref[pl.ds(r * tiles + t, 1), :] = pot[pl.ds(near_ids[r][t], 1), :]
        mine = pot[pl.ds(group + blk * local + r, 1), :]
        tail_ref[pl.ds(local * (tiles + 1) + r, 1), :] = jnp.where(lanes < own_kpt[r], dust + mine, 0.0)
    for sweep in range(ITERS):
        each_partner(lambda shift, member: mass_copy(sweep, shift, member).wait_send())
    for r in range(local):
        for t in range(tiles):
            base_copy(r, t).wait()


def finish(
    base_in, tail_in, plan_out, row_out, col_out, tail_ref, taken, made, in_sem, out_sem, end_sem
):
    local, tiles = base_in.shape[:2]
    places = [(r, t) for r in range(local) for t in range(tiles)]

    def fetch(r, t):
        return pltpu.make_async_copy(base_in.at[r, t], taken.at[r, t], in_sem.at[r, t])

    def put(r, t):
        return pltpu.make_async_copy(made.at[r, t], plan_out.at[r, t], out_sem.at[r, t])

    head = pltpu.make_async_copy(tail_in, tail_ref, end_sem.at[0])
    head.start()
    for place in places:
        fetch(*place).start()
    head.wait()
    ends = [
        pltpu.make_async_copy(
            tail_ref.at[pl.ds(local * (tiles + step), local)], target, end_sem.at[1 + step]
        )
        for step, target in enumerate((row_out, col_out))
    ]
    for end in ends:
        end.start()
    for r, t in places:
        fetch(r, t).wait()
        base = taken[r, t]
        out = base + tail_ref[pl.ds(r * tiles + t, 1), :]
        made[r, t] = jnp.where(base > 0.1 * DEAD, out, 0.0)
        put(r, t).start()
    for place in places:
        put(*place).wait()
    for end in ends:
        end.wait()


def on_device(
    img_count,
    blk_count,
    descriptors,
    covisible,
    tile_counts,
    keypoints,
    query_weight,
    key_weight,
    value_weight,
    merge_weight,
    output_weight,
    dustbin,
):
    local, block, width = descriptors.shape
    tiles = covisible.shape[1]
    group = local * blk_count
    near = 3 * group
    vmem = pl.BlockSpec(memory_space=pltpu.VMEM)
    hbm = pl.BlockSpec(memory_space=pltpu.HBM)
    dma = pltpu.SemaphoreType.DMA
    half = jnp.bfloat16
    full = jnp.float32
    base, tail = pl.pallas_call(
        functools.partial(kernel, img_count, blk_count),
        out_shape=(
            jax.ShapeDtypeStruct((local, tiles, block, block), full),
            jax.ShapeDtypeStruct((local * (tiles + 2), block), full),
        ),
        in_specs=[hbm] * 10,
        out_specs=(hbm, vmem),
        scratch_shapes=[
            pltpu.VMEM(descriptors.shape, half),
            pltpu.SMEM(covisible.shape, jnp.int32),
            pltpu.SMEM(tile_counts.shape, jnp.int32),
            pltpu.SMEM(keypoints.shape, jnp.int32),
            pltpu.VMEM(query_weight.shape, half),
            pltpu.VMEM(key_weight.shape, half),
            pltpu.VMEM(value_weight.shape, half),
            pltpu.VMEM(merge_weight.shape, half),
            pltpu.VMEM(output_weight.shape, half),
            pltpu.SMEM(dustbin.shape, full),
            dma((10,)),
            dma((descriptors.shape[0], tiles)),
            pltpu.VMEM((near, block, width), half),
            pltpu.VMEM((near, block, width), half),
            pltpu.VMEM((near, block, width), half),
            pltpu.VMEM((near, block, width), half),
            pltpu.VMEM((local, block, width), half),
            pltpu.VMEM((local, block, merge_weight.shape[1]), full),
            pltpu.VMEM((local, tiles, block, block), full),
            pltpu.VMEM((ITERS, 3, group, block), full),
            pltpu.VMEM((ITERS, 5, blk_count, 3, group, block), full),
            pltpu.VMEM((near, block), full),
            dma((3, blk_count)),
            dma((3, blk_count)),
            dma((3, blk_count)),
            dma((3, blk_count)),
            dma((ITERS, 5, blk_count)),
            dma((ITERS, 5, blk_count)),
        ],
        compiler_params=pltpu.CompilerParams(
            collective_id=0, has_side_effects=True
        ),
    )(
        descriptors,
        covisible,
        tile_counts,
        keypoints,
        query_weight,
        key_weight,
        value_weight,
        merge_weight,
        output_weight,
        dustbin,
    )
    return pl.pallas_call(
        finish,
        out_shape=(
            jax.ShapeDtypeStruct(base.shape, full),
            jax.ShapeDtypeStruct((local, block), full),
            jax.ShapeDtypeStruct((local, block), full),
        ),
        in_specs=[hbm, hbm],
        out_specs=(hbm, hbm, hbm),
        scratch_shapes=[
            pltpu.VMEM(tail.shape, full),
            pltpu.VMEM(base.shape, full),
            pltpu.VMEM(base.shape, full),
            dma((local, tiles)),
            dma((local, tiles)),
            dma((3,)),
        ],
    )(base, tail)


def solution(mesh):
    in_specs = (
        P(("img", "blk"), None, None),
        P(("img", "blk"), None),
        P(("img", "blk")),
        P(),
        P(),
        P(),
        P(),
        P(),
        P(),
        P(),
    )
    out_specs = (
        P(("img", "blk"), None, None, None),
        P(("img", "blk"), None),
        P(("img", "blk"), None),
    )
    return jax.shard_map(
        functools.partial(on_device, mesh.shape["img"], mesh.shape["blk"]),
        mesh=mesh,
        in_specs=in_specs,
        out_specs=out_specs,
        check_vma=False,
    )
```
